32 devices in a mesh: row: 4 (over y, x), col: 8 (over z, core).
Axes of the slice: x: 2, y: 2, z: 4, core: 2. Of those that a mesh axis runs over, the one named last changes fastest.
Arguments:
- targets: float32 [2, 16384], P(None, ('row', 'col')), may hold values from 0 to 1
- sources: bfloat16 [2, 16384], P(None, 'col'), may hold values from 0 to 1
- omega: bfloat16 [256, 16384], P(None, 'col'), may hold values from -0.046875 to 0.046875
- tree_order: int32 [16384], P(('row', 'col')), may hold values from 0 to 16383, each once
- leaf_pivots: int32 [32, 128], P(('row', 'col')), may hold values from 0 to 511, all different within a row
- pivots_one: int32 [16, 128], replicated, may hold values from 0 to 255, all different within a row
- pivots_two: int32 [8, 128], replicated, may hold values from 0 to 255, all different within a row
- pivots_three: int32 [4, 128], replicated, may hold values from 0 to 255, all different within a row
Outputs:
- leaf_interp: float32 [16384, 128], P(('row', 'col'))
- level_one_interp: float32 [4096, 128], P(('row', 'col'))
- level_two_interp: float32 [2048, 128], P(('row', 'col'))
- level_three_interp: float32 [1024, 128], P(('row', 'col'))
- root_sketch: float32 [512, 256], P(('row', 'col'))
The draws below stay inside these ranges and needn't reach their ends.
Inputs may be any that keep to these rules, and one draw needn't show every extreme that they name: tree_order names every target point once. `leaf_pivots`: each row names 128 distinct positions. `pivots_one`: each row names 128 distinct positions. `pivots_two`: each row names 128 distinct positions. `pivots_three`: each row names 128 distinct positions.
All inputs are finite; a program needn't handle non-finite values.
Results may differ from the reference program's by a relative error of at most 0.0074.
Values may be sent and summed in bfloat16 or wider, within the bound.
A program may use at most 192 MiB of HBM per device.

```python
import jax
import jax.numpy as jnp
from jax import lax

LEAF = 512
K = 128
S = 256
N = 16384
P_SIZE = 16384
NODES1 = 16
NODES2 = 8
NODES3 = 4


def level_of(own_key, extent, cuts, low, largest):
    def one(dim, blocks):
        heights = jax.random.uniform(jax.random.fold_in(jax.random.fold_in(own_key, 6), dim), (blocks,), jnp.float32, low / len(cuts), largest / len(cuts))
        return jnp.repeat(jnp.exp(heights), extent[dim] // blocks).reshape((-1,) + (1,) * (len(extent) - dim - 1))

    loudness = one(*cuts[0])
    for cut in cuts[1:]:
        loudness = loudness * one(*cut)
    return loudness


def choose_distinct(stream_key, rows, amount, top, lift):
    ranking = jax.random.permutation(jax.random.fold_in(stream_key, 1), amount)
    favour = ranking
    for power in range(3):
        favour = favour * favour // amount
    favour = favour * lift // amount
    chance = jax.random.randint(jax.random.fold_in(stream_key, 2), (rows, amount), 0, 4096) + favour
    sure = jax.random.permutation(jax.random.fold_in(stream_key, 3), rows)[jnp.arange(amount) % rows]
    chance = jnp.where(jnp.arange(rows)[:, None] == sure[None, :], 1 << 14, chance)
    priority = chance * amount + jnp.arange(amount)
    return lax.top_k(priority.astype(jnp.int32), top)[1].astype(jnp.int32)


def bell_draw(stream_key, dims, deviation, bound, cuts=(), held_as=jnp.bfloat16):
    array = jax.random.normal(stream_key, dims, jnp.float32) * deviation
    if len(cuts) > 0:
        array = level_of(stream_key, dims, cuts, -0.22, 0.18) * array
    return jnp.clip(array, min=-bound, max=bound).astype(held_as)


def setup_inputs(seed: int = 0) -> dict:
    key_of = jax.random.split(jax.random.key(seed), 9)
    targets = jnp.clip(1.0 * jax.random.uniform(key_of[0], (2, N), jnp.float32) ** level_of(key_of[0], (2, N), ((1, 32),), -0.2, 0.2), 0.0, 1.0)
    sources = jnp.clip(1.0 * jax.random.uniform(key_of[1], (2, P_SIZE), jnp.float32) ** level_of(key_of[1], (2, P_SIZE), ((1, 8),), -0.2, 0.2), 0.0, 1.0).astype(jnp.bfloat16)
    omega = bell_draw(key_of[2], (S, P_SIZE), P_SIZE ** -0.5, 0.046875, ((1, 8),))
    tree_order = jax.random.permutation(key_of[3], N).astype(jnp.int32)
    leaf_pivots = choose_distinct(key_of[4], (N // LEAF), LEAF, K, 0)
    pivots_one = choose_distinct(key_of[5], NODES1, 2 * K, K, 0)
    pivots_two = choose_distinct(key_of[6], NODES2, 2 * K, K, 0)
    pivots_three = choose_distinct(key_of[7], NODES3, 2 * K, K, 0)
    return {"targets": targets, "sources": sources, "omega": omega, "tree_order": tree_order, "leaf_pivots": leaf_pivots, "pivots_one": pivots_one, "pivots_two": pivots_two, "pivots_three": pivots_three}


RIDGE = 0.1
DELTA_SQUARED = 0.0001

def kernel_block(points, source_pts):
    delta_x = points[0][:, None] - source_pts[0][None, :].astype(jnp.float32)
    delta_y = points[1][:, None] - source_pts[1][None, :].astype(jnp.float32)
    return (-0.5 * jnp.log(delta_x * delta_x + delta_y * delta_y + DELTA_SQUARED)).astype(jnp.bfloat16)

def select_factor(candidates, pivots):
    chosen = jnp.take(candidates, pivots, axis=0)
    gram_matrix = jnp.dot(chosen, chosen.T, precision=lax.Precision.HIGHEST)
    ridge_shift = RIDGE * (jnp.trace(gram_matrix) / chosen.shape[0] + 1e-06)
    shifted = gram_matrix + ridge_shift * jnp.eye(chosen.shape[0], dtype=gram_matrix.dtype)
    return (chosen, jnp.linalg.cholesky(shifted))

def solve_rows(chosen, factor, row_block):
    right_side = jnp.dot(chosen, row_block.T, precision=lax.Precision.HIGHEST)
    first = lax.linalg.triangular_solve(factor, right_side, left_side=True, lower=True)
    second = lax.linalg.triangular_solve(factor, first, left_side=True, lower=True, transpose_a=True)
    return second.T

def reference(targets, sources, omega, tree_order, leaf_pivots, pivots_one, pivots_two, pivots_three):
    placed = jnp.take(targets, tree_order, axis=1)
    blocks = placed.reshape(2, N // LEAF, LEAF).transpose(1, 0, 2)

    def sketch_block(block):
        panel = kernel_block(block, sources)
        return lax.dot_general(panel.astype(jnp.float32), omega.astype(jnp.float32), (((1,), (1,)), ((), ())), preferred_element_type=jnp.float32)
    leaf_sketches = lax.map(sketch_block, blocks)
    chosen, factors = jax.vmap(select_factor)(leaf_sketches, leaf_pivots)
    results = [jax.vmap(solve_rows)(chosen, factors, leaf_sketches).reshape(N, K)]
    for pivot_table in (pivots_one, pivots_two, pivots_three):
        candidates = chosen.reshape(-1, 2 * K, S)
        chosen, factors = jax.vmap(select_factor)(candidates, pivot_table)
        results.append(jax.vmap(solve_rows)(chosen, factors, candidates).reshape(-1, K))
    return (results[0], results[1], results[2], results[3], chosen.reshape(-1, S))
```

```python
import functools

import jax
import jax.numpy as jnp
from jax import lax
from jax.experimental import pallas as pl
from jax.experimental.pallas import tpu as pltpu
from jax.sharding import PartitionSpec as P

RIDGE = 0.1
DELTA_SQUARED = 0.0001
LEVELS = 3
LANES = 128
CHUNK = 512
MESH = pl.DeviceIdType.MESH
HIGHEST = lax.Precision.HIGHEST
F32 = jnp.float32
BF16 = jnp.bfloat16


def split3(x):
    a = x.astype(BF16)
    r = x - a.astype(F32)
    b = r.astype(BF16)
    c = (r - b.astype(F32)).astype(BF16)
    return a, b, c


def pick_columns(pieces, pivots):
    m = pieces[0].shape[1]
    hot = (
        lax.broadcasted_iota(jnp.int32, (m, pivots.shape[1]), 0) == pivots
    ).astype(F32).astype(BF16)
    out = None
    for piece in pieces:
        term = jnp.dot(piece, hot, preferred_element_type=F32)
        out = term if out is None else out + term
    return out


def sketch_kernel(
    rows, cols,
    tgt_ref, src_ref, om_ref, ord_ref, leaf_ref, p1_ref, p2_ref, p3_ref,
    sk_ref, ch_ref,
    every, orders, table, acc, part_out, part_in, z_out, z_in, ex_out, ex_in,
    tgt_send, tgt_recv, ord_send, ord_recv, part_send, part_recv, z_send, z_recv, ex_send, ex_recv,
):
    n = rows * cols
    zs = cols // 2
    row = lax.axis_index("row")
    col = lax.axis_index("col")
    me = row * cols + col
    z = col // 2
    core = col % 2
    partner = z * 2 + (1 - core)
    length = ord_ref.shape[1]
    per = tgt_ref.shape[0]

    barrier = pltpu.get_barrier_semaphore()

    def greet(i, carry):
        other = lax.rem(me + i, n)
        pl.semaphore_signal(
            barrier, inc=1, device_id=(other // cols, other % cols), device_id_type=MESH
        )
        return carry

    lax.fori_loop(1, n, greet, 0)
    pl.semaphore_wait(barrier, n - 1)

    def tgt_copy(i):
        other = lax.rem(me + i, n)
        return pltpu.make_async_remote_copy(
            src_ref=tgt_ref, dst_ref=every.at[me],
            send_sem=tgt_send.at[i], recv_sem=tgt_recv.at[i],
            device_id=(other // cols, other % cols), device_id_type=MESH,
        )

    def ord_copy(i):
        other = lax.rem(col + i, cols)
        return pltpu.make_async_remote_copy(
            src_ref=ord_ref, dst_ref=orders.at[col],
            send_sem=ord_send.at[i], recv_sem=ord_recv.at[i],
            device_id=(row, other), device_id_type=MESH,
        )

    def start(copy):
        def go(i, carry):
            copy(i).start()
            return carry
        return go

    def finish(copy):
        def go(i, carry):
            copy(i).wait()
            return carry
        return go

    lax.fori_loop(1, n, start(tgt_copy), 0)
    lax.fori_loop(1, cols, start(ord_copy), 0)
    every[me] = tgt_ref[...]
    orders[col] = ord_ref[...]
    lax.fori_loop(1, n, finish(tgt_copy), 0)
    lax.fori_loop(1, cols, finish(ord_copy), 0)

    flat = every[...].reshape(n * per, LANES).T
    for i, piece in enumerate(split3(flat)):
        table[i] = piece

    half = per // 2

    def points_of(leaf):
        order = orders[leaf]
        owner_row = order // (half * LANES) * per + order // LANES % half
        lane = order % LANES
        rows_iota = lax.broadcasted_iota(jnp.int32, (n * per, length), 0)
        lane_iota = lax.broadcasted_iota(jnp.int32, (LANES, length), 0)
        out = []
        for c in range(2):
            hot = (rows_iota == owner_row + c * half).astype(F32).astype(BF16)
            got = jnp.dot(table[0], hot, preferred_element_type=F32)
            got += jnp.dot(table[1], hot, preferred_element_type=F32)
            got += jnp.dot(table[2], hot, preferred_element_type=F32)
            out.append(jnp.sum(jnp.where(lane_iota == lane, got, 0.0), axis=0, keepdims=True))
        return out

    sources = src_ref.shape[0]

    def block(leaf):
        px, py = points_of(leaf)
        acc[...] = jnp.zeros_like(acc)

        def chunk(i, carry):
            at = pl.multiple_of(i * CHUNK, CHUNK)
            s = src_ref[pl.ds(at, CHUNK), :]
            dx = px - s[:, 0:1]
            dy = py - s[:, 1:2]
            panel = (-0.5 * jnp.log(dx * dx + dy * dy + DELTA_SQUARED)).astype(BF16)
            acc[...] += jnp.dot(
                om_ref[:, pl.ds(at, CHUNK)], panel, preferred_element_type=F32
            )
            return carry

        lax.fori_loop(0, sources // CHUNK, chunk, 0)

    def part_copy(k):
        return pltpu.make_async_remote_copy(
            src_ref=part_out.at[k], dst_ref=part_in.at[k],
            send_sem=part_send.at[k], recv_sem=part_recv.at[k],
            device_id=(row, partner), device_id_type=MESH,
        )

    def z_copy(k):
        to = lax.rem(z + k, zs)
        return pltpu.make_async_remote_copy(
            src_ref=z_out.at[k], dst_ref=z_in.at[k],
            send_sem=z_send.at[k], recv_sem=z_recv.at[k],
            device_id=(row, to * 2 + core), device_id_type=MESH,
        )

    def both(k):
        to = lax.rem(z + k, zs)
        block(to * 2 + (1 - core))
        part_out[k] = acc[...].astype(BF16)
        part_copy(k).start()
        block(to * 2 + core)
        part_copy(k).wait()

    def step(k, carry):
        both(k)
        z_out[k] = (acc[...] + part_in[k].astype(F32)).astype(BF16)
        z_copy(k).start()
        return carry

    lax.fori_loop(1, zs, step, 0)
    both(0)
    acc[...] += part_in[0].astype(F32)

    def collect(k, carry):
        z_copy(k).wait()
        acc[...] += z_in[k].astype(F32)
        return carry

    lax.fori_loop(1, zs, collect, 0)

    sk_ref[...] = acc[...]
    chosen = pick_columns(split3(acc[...]), leaf_ref[...])
    ch_ref[0] = chosen
    for s, p_ref in enumerate((p1_ref, p2_ref, p3_ref)):
        bit = col // 2**s % 2
        other = col + (1 - 2 * bit) * 2**s
        ex_out[s] = chosen
        copy = pltpu.make_async_remote_copy(
            src_ref=ex_out.at[s], dst_ref=ex_in.at[s],
            send_sem=ex_send.at[s], recv_sem=ex_recv.at[s],
            device_id=(row, other), device_id_type=MESH,
        )
        copy.start()
        copy.wait()
        theirs = ex_in[s]
        high = bit == 1
        low_part = jnp.where(high, theirs, chosen)
        high_part = jnp.where(high, chosen, theirs)
        cand = jnp.concatenate([low_part, high_part], axis=1)
        chosen = pick_columns(split3(cand), p_ref[pl.ds(me // 2 ** (s + 1), 1), :])
        ch_ref[s + 1] = chosen


def contract0(a, b):
    return lax.dot_general(
        a, b, (((0,), (0,)), ((), ())), precision=HIGHEST, preferred_element_type=F32
    )


def solve_kernel(sk_ref, ch_ref, o0, o1, o2, o3, root, a_ref, r_ref, t_ref):
    col = lax.axis_index("col")
    k = ch_ref.shape[2]
    levels = ch_ref.shape[0]
    lane2 = lax.broadcasted_iota(jnp.int32, (k, k), 1)
    sub2 = lax.broadcasted_iota(jnp.int32, (k, k), 0)
    for m in range(levels):
        gram = contract0(ch_ref[m], ch_ref[m])
        eye = lane2 == sub2
        trace = jnp.sum(jnp.where(eye, gram, 0.0))
        shift = RIDGE * (trace / k + 1e-06)
        a_ref[m] = gram + jnp.where(eye, shift, 0.0)

    lane1 = lax.broadcasted_iota(jnp.int32, (1, k), 1)

    def step(i, carry):
        here = lane2 == i
        here1 = lane1 == i
        for m in range(levels):
            a = a_ref[m]
            r = a_ref[m, pl.ds(i, 1), :]
            c = jnp.sum(jnp.where(here, a, 0.0), axis=1, keepdims=True)
            p = 1.0 / jnp.sum(jnp.where(here1, r, 0.0), axis=1, keepdims=True)
            rp = jnp.where(here1, p, r * p)
            a_ref[m] = jnp.where(here, 0.0, a) - c * rp
            a_ref[m, pl.ds(i, 1), :] = rp
        return carry

    lax.fori_loop(0, k, step, 0)
    right = contract0(sk_ref[...], ch_ref[0])
    o0[...] = jnp.dot(right, a_ref[0], precision=HIGHEST, preferred_element_type=F32)
    for s, o in enumerate((o1, o2, o3)):
        r_ref[...] = contract0(ch_ref[s], ch_ref[s + 1])
        size = o.shape[0]
        at = pl.multiple_of(col % 2**s * size, size)
        o[...] = jnp.dot(
            r_ref[pl.ds(at, size), :], a_ref[s + 1], precision=HIGHEST,
            preferred_element_type=F32,
        )
    t_ref[...] = ch_ref[levels - 1].T
    size = root.shape[0]
    root[...] = t_ref[pl.ds(pl.multiple_of(col % 2**LEVELS * size, size), size), :]


def body(rows, cols, targets, sources, omega, tree_order, leaf_pivots, p1, p2, p3):
    n = rows * cols
    zs = cols // 2
    leaf = tree_order.shape[0]
    width = omega.shape[0]
    k = leaf_pivots.shape[1]
    per = targets.size // LANES
    vmem = pl.BlockSpec(memory_space=pltpu.VMEM)
    dma = lambda *d: pltpu.SemaphoreType.DMA(d)
    sketch, chosen = pl.pallas_call(
        functools.partial(sketch_kernel, rows, cols),
        out_shape=(
            jax.ShapeDtypeStruct((width, leaf), F32),
            jax.ShapeDtypeStruct((LEVELS + 1, width, k), F32),
        ),
        in_specs=[vmem] * 8,
        out_specs=(vmem, vmem),
        scratch_shapes=[
            pltpu.VMEM((n, per, LANES), F32),
            pltpu.VMEM((cols, 1, leaf), jnp.int32),
            pltpu.VMEM((3, LANES, n * per), BF16),
            pltpu.VMEM((width, leaf), F32),
            pltpu.VMEM((zs, width, leaf), BF16),
            pltpu.VMEM((zs, width, leaf), BF16),
            pltpu.VMEM((zs, width, leaf), BF16),
            pltpu.VMEM((zs, width, leaf), BF16),
            pltpu.VMEM((LEVELS, width, k), F32),
            pltpu.VMEM((LEVELS, width, k), F32),
            dma(n), dma(n), dma(cols), dma(cols), dma(zs), dma(zs), dma(zs), dma(zs),
            dma(LEVELS), dma(LEVELS),
        ],
        compiler_params=pltpu.CompilerParams(
            collective_id=0, has_side_effects=True, vmem_limit_bytes=48 << 20
        ),
    )(
        targets.reshape(per, LANES),
        sources.astype(F32).T,
        omega,
        tree_order.reshape(1, leaf),
        leaf_pivots,
        p1, p2, p3,
    )
    out_rows = [leaf] + [k // 2**s for s in range(LEVELS)]
    return pl.pallas_call(
        solve_kernel,
        out_shape=tuple(jax.ShapeDtypeStruct((r, k), F32) for r in out_rows)
        + (jax.ShapeDtypeStruct((k // 2**LEVELS, width), F32),),
        in_specs=[vmem, vmem],
        out_specs=(vmem,) * (len(out_rows) + 1),
        scratch_shapes=[
            pltpu.VMEM((LEVELS + 1, k, k), F32),
            pltpu.VMEM((k, k), F32),
            pltpu.VMEM((k, width), F32),
        ],
        compiler_params=pltpu.CompilerParams(vmem_limit_bytes=32 << 20),
    )(sketch, chosen)


def solution(mesh):
    both = P(("row", "col"), None)
    return jax.shard_map(
        functools.partial(body, mesh.shape["row"], mesh.shape["col"]),
        mesh=mesh,
        in_specs=(
            P(None, ("row", "col")),
            P(None, "col"),
            P(None, "col"),
            P(("row", "col")),
            both,
            P(),
            P(),
            P(),
        ),
        out_specs=(both,) * 5,
        check_vma=False,
    )
```

```python
import functools

import jax
import jax.numpy as jnp
from jax import lax
from jax.experimental import pallas as pl
from jax.experimental.pallas import tpu as pltpu
from jax.sharding import PartitionSpec as P

RIDGE = 0.1
DELTA_SQUARED = 0.0001
LEVELS = 3
LANES = 128
CHUNK = 256
LN2 = 0.6931471805599453
MESH = pl.DeviceIdType.MESH
HIGHEST = lax.Precision.HIGHEST
F32 = jnp.float32
BF16 = jnp.bfloat16


def split3(x):
    a = x.astype(BF16)
    r = x - a.astype(F32)
    b = r.astype(BF16)
    c = (r - b.astype(F32)).astype(BF16)
    return a, b, c


def pick_columns(pieces, pivots):
    m = pieces[0].shape[1]
    hot = (
        lax.broadcasted_iota(jnp.int32, (m, pivots.shape[1]), 0) == pivots
    ).astype(F32).astype(BF16)
    out = None
    for piece in pieces:
        term = jnp.dot(piece, hot, preferred_element_type=F32)
        out = term if out is None else out + term
    return out


def sketch_kernel(
    rows, cols,
    tgt_ref, src_ref, om_ref, ord_ref, leaf_ref, p1_ref, p2_ref, p3_ref,
    sk_ref, ch_ref,
    every, orders, table, src_col, acc, part_out, part_in, z_out, z_in, ex_out, ex_in,
    tgt_send, tgt_recv, ord_send, ord_recv, part_send, part_recv, z_send, z_recv, ex_send, ex_recv,
):
    n = rows * cols
    zs = cols // 2
    row = lax.axis_index("row")
    col = lax.axis_index("col")
    me = row * cols + col
    z = col // 2
    core = col % 2
    partner = z * 2 + (1 - core)
    length = ord_ref.shape[1]
    local = tgt_ref.shape[1]
    per = 2 * local // LANES

    barrier = pltpu.get_barrier_semaphore()

    def greet(i, carry):
        other = lax.rem(me + i, n)
        pl.semaphore_signal(
            barrier, inc=1, device_id=(other // cols, other % cols), device_id_type=MESH
        )
        return carry

    lax.fori_loop(1, n, greet, 0)
    pl.semaphore_wait(barrier, n - 1)

    def tgt_copy(i):
        other = lax.rem(me + i, n)
        return pltpu.make_async_remote_copy(
            src_ref=tgt_ref, dst_ref=every.at[me],
            send_sem=tgt_send.at[i], recv_sem=tgt_recv.at[i],
            device_id=(other // cols, other % cols), device_id_type=MESH,
        )

    def ord_copy(i):
        other = lax.rem(col + i, cols)
        return pltpu.make_async_remote_copy(
            src_ref=ord_ref, dst_ref=orders.at[col],
            send_sem=ord_send.at[i], recv_sem=ord_recv.at[i],
            device_id=(row, other), device_id_type=MESH,
        )

    def start(copy):
        def go(i, carry):
            copy(i).start()
            return carry
        return go

    def finish(copy):
        def go(i, carry):
            copy(i).wait()
            return carry
        return go

    lax.fori_loop(1, n, start(tgt_copy), 0)
    lax.fori_loop(1, cols, start(ord_copy), 0)
    every[me] = tgt_ref[...]
    orders[col] = ord_ref[...]
    wide = src_ref[...].astype(F32)
    src_col[...] = jnp.concatenate([wide, jnp.zeros((6, wide.shape[1]), F32)], axis=0).T
    lax.fori_loop(1, n, finish(tgt_copy), 0)
    lax.fori_loop(1, cols, finish(ord_copy), 0)

    flat = jnp.concatenate(
        [
            every[:, c, a * LANES : (a + 1) * LANES]
            for a in range(local // LANES)
            for c in range(2)
        ],
        axis=0,
    ).T
    for i, piece in enumerate(split3(flat)):
        table[i] = piece

    def points_of(leaf):
        order = orders[leaf]
        owner_row = order // LANES % (local // LANES) * (2 * n) + order // local
        lane = order % LANES
        rows_iota = lax.broadcasted_iota(jnp.int32, (n * per, length), 0)
        lane_iota = lax.broadcasted_iota(jnp.int32, (LANES, length), 0)
        out = []
        for c in range(2):
            hot = (rows_iota == owner_row + c * n).astype(F32).astype(BF16)
            got = jnp.dot(table[0], hot, preferred_element_type=F32)
            got += jnp.dot(table[1], hot, preferred_element_type=F32)
            got += jnp.dot(table[2], hot, preferred_element_type=F32)
            out.append(jnp.sum(jnp.where(lane_iota == lane, got, 0.0), axis=0, keepdims=True))
        return out

    sources = src_ref.shape[1]

    def block(leaf):
        px, py = points_of(leaf)
        total = None
        for at in range(0, sources, CHUNK):
            s = src_col[at : at + CHUNK, :]
            dx = px - s[:, 0:1]
            dy = py - s[:, 1:2]
            panel = (-0.5 * LN2) * jnp.log2(dx * dx + dy * dy + DELTA_SQUARED)
            term = jnp.dot(
                om_ref[:, at : at + CHUNK], panel.astype(BF16), preferred_element_type=F32
            )
            total = term if total is None else total + term
        acc[...] = total

    def part_copy(k):
        return pltpu.make_async_remote_copy(
            src_ref=part_out.at[k], dst_ref=part_in.at[k],
            send_sem=part_send.at[k], recv_sem=part_recv.at[k],
            device_id=(row, partner), device_id_type=MESH,
        )

    def z_copy(k):
        to = lax.rem(z + k, zs)
        return pltpu.make_async_remote_copy(
            src_ref=z_out.at[k], dst_ref=z_in.at[k],
            send_sem=z_send.at[k], recv_sem=z_recv.at[k],
            device_id=(row, to * 2 + core), device_id_type=MESH,
        )

    def both(k):
        to = lax.rem(z + k, zs)
        block(to * 2 + (1 - core))
        part_out[k] = acc[...].astype(BF16)
        part_copy(k).start()
        block(to * 2 + core)
        part_copy(k).wait()

    def step(k, carry):
        both(k)
        z_out[k] = (acc[...] + part_in[k].astype(F32)).astype(BF16)
        z_copy(k).start()
        return carry

    lax.fori_loop(1, zs, step, 0)
    both(0)
    acc[...] += part_in[0].astype(F32)

    def collect(k, carry):
        z_copy(k).wait()
        acc[...] += z_in[k].astype(F32)
        return carry

    lax.fori_loop(1, zs, collect, 0)

    sk_ref[...] = acc[...]
    chosen = pick_columns(split3(acc[...]), leaf_ref[...])
    ch_ref[0] = chosen
    for s, p_ref in enumerate((p1_ref, p2_ref, p3_ref)):
        bit = col // 2**s % 2
        other = col + (1 - 2 * bit) * 2**s
        ex_out[s] = chosen
        copy = pltpu.make_async_remote_copy(
            src_ref=ex_out.at[s], dst_ref=ex_in.at[s],
            send_sem=ex_send.at[s], recv_sem=ex_recv.at[s],
            device_id=(row, other), device_id_type=MESH,
        )
        copy.start()
        copy.wait()
        theirs = ex_in[s]
        high = bit == 1
        low_part = jnp.where(high, theirs, chosen)
        high_part = jnp.where(high, chosen, theirs)
        cand = jnp.concatenate([low_part, high_part], axis=1)
        chosen = pick_columns(split3(cand), p_ref[pl.ds(me // 2 ** (s + 1), 1), :])
        ch_ref[s + 1] = chosen


def contract0(a, b):
    return lax.dot_general(
        a, b, (((0,), (0,)), ((), ())), precision=HIGHEST, preferred_element_type=F32
    )


def halves(x):
    h = x.astype(BF16)
    return h, (x - h.astype(F32)).astype(BF16)


def product3(a, b):
    ah, al = halves(a)
    bh, bl = halves(b)
    dot = functools.partial(jnp.dot, preferred_element_type=F32)
    return dot(ah, bh) + (dot(ah, bl) + dot(al, bh))


def product6(a, b):
    return jnp.dot(a, b, precision=HIGHEST, preferred_element_type=F32)


def shifted_inverses(grams):
    k = grams[0].shape[0]
    eye = lax.broadcasted_iota(jnp.int32, (k, k), 0) == lax.broadcasted_iota(
        jnp.int32, (k, k), 1
    )
    one = jnp.where(eye, 1.0, 0.0)
    low = 1.0 / (k / RIDGE + 1.0)
    gap = (1.0 - low) / (1.0 + low)
    first = 2.0 / (1.0 + low)
    tops, mats = [], []
    for gram in grams:
        trace = jnp.sum(jnp.where(eye, gram, 0.0), axis=(0, 1), keepdims=True)
        shift = RIDGE * (trace / k + 1e-06)
        tops.append(trace + shift)
        mats.append((gram + shift * one) / (trace + shift))
    scale = 2.0 / (2.0 - gap * gap)
    xs = [scale * (2.0 * first * one - first * first * m) for m in mats]
    gap = gap * gap / (2.0 - gap * gap)
    scales = []
    while gap > 1e-9:
        scales.append(2.0 / (2.0 - gap * gap))
        gap = gap * gap / (2.0 - gap * gap)
    for i, scale in enumerate(scales):
        product = product6 if i >= len(scales) - 2 else product3
        ys = [scale * (2.0 * one - product(m, x)) for m, x in zip(mats, xs)]
        xs = [product(x, y) for x, y in zip(xs, ys)]
    return [x / t for x, t in zip(xs, tops)]


def solve_kernel(sk_ref, ch_ref, o0, o1, o2, o3, root, r_ref, t_ref):
    col = lax.axis_index("col")
    levels = ch_ref.shape[0]
    inverse = shifted_inverses([contract0(ch_ref[m], ch_ref[m]) for m in range(levels)])
    o0[...] = product6(contract0(sk_ref[...], ch_ref[0]), inverse[0])
    for s, o in enumerate((o1, o2, o3)):
        r_ref[...] = contract0(ch_ref[s], ch_ref[s + 1])
        size = o.shape[0]
        at = pl.multiple_of(col % 2**s * size, size)
        o[...] = product6(r_ref[pl.ds(at, size), :], inverse[s + 1])
    t_ref[...] = ch_ref[levels - 1].T
    size = root.shape[0]
    root[...] = t_ref[pl.ds(pl.multiple_of(col % 2**LEVELS * size, size), size), :]


def body(rows, cols, targets, sources, omega, tree_order, leaf_pivots, p1, p2, p3):
    n = rows * cols
    zs = cols // 2
    leaf = tree_order.shape[0]
    width = omega.shape[0]
    k = leaf_pivots.shape[1]
    per = targets.size // LANES
    vmem = pl.BlockSpec(memory_space=pltpu.VMEM)
    dma = lambda *d: pltpu.SemaphoreType.DMA(d)
    sketch, chosen = pl.pallas_call(
        functools.partial(sketch_kernel, rows, cols),
        out_shape=(
            jax.ShapeDtypeStruct((width, leaf), F32),
            jax.ShapeDtypeStruct((LEVELS + 1, width, k), F32),
        ),
        in_specs=[vmem] * 8,
        out_specs=(vmem, vmem),
        scratch_shapes=[
            pltpu.VMEM((n, 2, leaf), F32),
            pltpu.VMEM((cols, 1, leaf), jnp.int32),
            pltpu.VMEM((3, LANES, n * per), BF16),
            pltpu.VMEM((sources.shape[1], 8), F32),
            pltpu.VMEM((width, leaf), F32),
            pltpu.VMEM((zs, width, leaf), BF16),
            pltpu.VMEM((zs, width, leaf), BF16),
            pltpu.VMEM((zs, width, leaf), BF16),
            pltpu.VMEM((zs, width, leaf), BF16),
            pltpu.VMEM((LEVELS, width, k), F32),
            pltpu.VMEM((LEVELS, width, k), F32),
            dma(n), dma(n), dma(cols), dma(cols), dma(zs), dma(zs), dma(zs), dma(zs),
            dma(LEVELS), dma(LEVELS),
        ],
        compiler_params=pltpu.CompilerParams(
            collective_id=0, has_side_effects=True, vmem_limit_bytes=48 << 20
        ),
    )(
        targets,
        sources,
        omega,
        tree_order.reshape(1, leaf),
        leaf_pivots,
        p1, p2, p3,
    )
    out_rows = [leaf] + [k // 2**s for s in range(LEVELS)]
    return pl.pallas_call(
        solve_kernel,
        out_shape=tuple(jax.ShapeDtypeStruct((r, k), F32) for r in out_rows)
        + (jax.ShapeDtypeStruct((k // 2**LEVELS, width), F32),),
        in_specs=[vmem, vmem],
        out_specs=(vmem,) * (len(out_rows) + 1),
        scratch_shapes=[
            pltpu.VMEM((k, k), F32),
            pltpu.VMEM((k, width), F32),
        ],
        compiler_params=pltpu.CompilerParams(vmem_limit_bytes=32 << 20),
    )(sketch, chosen)


def solution(mesh):
    both = P(("row", "col"), None)
    return jax.shard_map(
        functools.partial(body, mesh.shape["row"], mesh.shape["col"]),
        mesh=mesh,
        in_specs=(
            P(None, ("row", "col")),
            P(None, "col"),
            P(None, "col"),
            P(("row", "col")),
            both,
            P(),
            P(),
            P(),
        ),
        out_specs=(both,) * 5,
        check_vma=False,
    )
```

```python
import functools

import jax
import jax.numpy as jnp
from jax import lax
from jax.experimental import pallas as pl
from jax.experimental.pallas import tpu as pltpu
from jax.sharding import PartitionSpec as P

RIDGE = 0.1
DELTA_SQUARED = 0.0001
LEVELS = 3
LANES = 128
CHUNK = 512
SIDE = 24
LN2 = 0.6931471805599453
MESH = pl.DeviceIdType.MESH
HIGHEST = lax.Precision.HIGHEST
F32 = jnp.float32
BF16 = jnp.bfloat16


def split3(x):
    a = x.astype(BF16)
    r = x - a.astype(F32)
    b = r.astype(BF16)
    c = (r - b.astype(F32)).astype(BF16)
    return a, b, c


def pick_columns(pieces, pivots):
    m = pieces[0].shape[1]
    hot = (
        lax.broadcasted_iota(jnp.int32, (m, pivots.shape[1]), 0) == pivots
    ).astype(F32).astype(BF16)
    out = None
    for piece in pieces:
        term = jnp.dot(piece, hot, preferred_element_type=F32)
        out = term if out is None else out + term
    return out


def flip(value, mask, bits):
    out = 0
    for i in range(bits):
        out = out + (value // 2**i + mask // 2**i) % 2 * 2**i
    return out


def sketch_kernel(
    rows, cols,
    tgt_hbm, src_hbm, om_hbm, ord_hbm, leaf_hbm, p1_hbm, p2_hbm, p3_hbm,
    sk_ref, ch_ref, inv_ref,
    src_ref, om_ref, leaf_ref, p1_ref, p2_ref, p3_ref,
    every, orders, table, src_left, acc, part_out, part_in, z_out, z_in, ex_out, ex_in,
    load_sem,
    tgt_send, tgt_recv, ord_send, ord_recv, part_send, part_recv, z_send, z_recv,
    ex_send, ex_recv, pass_send, pass_recv,
):
    n = rows * cols
    zs = cols // 2
    bits = zs.bit_length() - 1
    row = lax.axis_index("row")
    col = lax.axis_index("col")
    me = row * cols + col
    z = col // 2
    core = col % 2
    partner = z * 2 + (1 - core)
    length = ord_hbm.shape[1]
    local = tgt_hbm.shape[1]
    per = 2 * local // LANES

    loads = [
        pltpu.make_async_copy(src, dst, load_sem.at[i])
        for i, (src, dst) in enumerate(
            (
                (src_hbm, src_ref), (om_hbm, om_ref), (leaf_hbm, leaf_ref),
                (p1_hbm, p1_ref), (p2_hbm, p2_ref), (p3_hbm, p3_ref),
                (tgt_hbm, every.at[me]), (ord_hbm, orders.at[col]),
            )
        )
    ]
    for load in loads:
        load.start()

    barrier = pltpu.get_barrier_semaphore()

    def greet(i, carry):
        other = lax.rem(me + i, n)
        pl.semaphore_signal(
            barrier, inc=1, device_id=(other // cols, other % cols), device_id_type=MESH
        )
        return carry

    lax.fori_loop(1, n, greet, 0)
    pl.semaphore_wait(barrier, n - 1)

    def tgt_copy(i):
        other = lax.rem(me + i, n)
        return pltpu.make_async_remote_copy(
            src_ref=tgt_hbm, dst_ref=every.at[me],
            send_sem=tgt_send.at[i], recv_sem=tgt_recv.at[i],
            device_id=(other // cols, other % cols), device_id_type=MESH,
        )

    def ord_copy(i):
        other = lax.rem(col + i, cols)
        return pltpu.make_async_remote_copy(
            src_ref=ord_hbm, dst_ref=orders.at[col],
            send_sem=ord_send.at[i], recv_sem=ord_recv.at[i],
            device_id=(row, other), device_id_type=MESH,
        )

    def start(copy):
        def go(i, carry):
            copy(i).start()
            return carry
        return go

    def finish(copy):
        def go(i, carry):
            copy(i).wait()
            return carry
        return go

    lax.fori_loop(1, n, start(tgt_copy), 0)
    lax.fori_loop(1, cols, start(ord_copy), 0)
    for load in loads:
        load.wait()

    def pieces(x):
        return [p.astype(F32) for p in split3(x)]

    wide = src_ref[...].astype(F32) - 0.5
    sx, sy = wide[0:1], wide[1:2]
    ones = jnp.ones_like(sx)
    left = []
    for part in (-2.0 * sx, -2.0 * sy):
        a, b, c = pieces(part)
        left += [a, a, a, b, b, c]
    left += pieces(sx * sx + sy * sy) + [ones] * 3
    left += [jnp.zeros_like(sx)] * (SIDE - len(left))
    src_left[...] = jnp.concatenate(left, axis=0).T.astype(BF16)

    lax.fori_loop(1, n, finish(tgt_copy), 0)
    lax.fori_loop(1, cols, finish(ord_copy), 0)

    flat = jnp.concatenate(
        [
            every[:, c, a * LANES : (a + 1) * LANES]
            for a in range(local // LANES)
            for c in range(2)
        ],
        axis=0,
    ).T
    for i, piece in enumerate(split3(flat)):
        table[i] = piece

    def points_of(leaf):
        order = orders[leaf]
        owner_row = order // LANES % (local // LANES) * (2 * n) + order // local
        lane = order % LANES
        rows_iota = lax.broadcasted_iota(jnp.int32, (n * per, length), 0)
        lane_iota = lax.broadcasted_iota(jnp.int32, (LANES, length), 0)
        out = []
        for c in range(2):
            hot = (rows_iota == owner_row + c * n).astype(F32).astype(BF16)
            got = jnp.dot(table[0], hot, preferred_element_type=F32)
            got += jnp.dot(table[1], hot, preferred_element_type=F32)
            got += jnp.dot(table[2], hot, preferred_element_type=F32)
            out.append(jnp.sum(jnp.where(lane_iota == lane, got, 0.0), axis=0, keepdims=True))
        return out

    sources = src_ref.shape[1]

    def block(leaf):
        px, py = points_of(leaf)
        px, py = px - 0.5, py - 0.5
        right = []
        for part in (px, py):
            a, b, c = pieces(part)
            right += [a, b, c, a, b, a]
        right += [jnp.ones_like(px)] * 3 + pieces(px * px + py * py + DELTA_SQUARED)
        right += [jnp.zeros_like(px)] * (SIDE - len(right))
        points = jnp.concatenate(right, axis=0).astype(BF16)

        def squares(at):
            return jnp.dot(
                src_left[at : at + CHUNK, :], points, preferred_element_type=F32
            )

        total = None
        ahead = squares(0)
        for at in range(0, sources, CHUNK):
            now = ahead
            if at + CHUNK < sources:
                ahead = squares(at + CHUNK)
            panel = ((-0.5 * LN2) * jnp.log2(now)).astype(BF16)
            term = jnp.dot(
                om_ref[:, at : at + CHUNK], panel, preferred_element_type=F32
            )
            total = term if total is None else total + term
        acc[...] = total

    def part_copy(x):
        return pltpu.make_async_remote_copy(
            src_ref=part_out.at[x], dst_ref=part_in.at[x],
            send_sem=part_send.at[x], recv_sem=part_recv.at[x],
            device_id=(row, partner), device_id_type=MESH,
        )

    def z_copy(x, b):
        return pltpu.make_async_remote_copy(
            src_ref=z_out.at[x], dst_ref=z_in.at[x],
            send_sem=z_send.at[x], recv_sem=z_recv.at[x],
            device_id=(row, flip(z, 2**b, bits) * 2 + core), device_id_type=MESH,
        )

    def both(x, received):
        to = flip(z, x, bits)
        block(to * 2 + (1 - core))
        part_out[x] = acc[...]
        part_copy(x).start()
        block(to * 2 + core)
        part_copy(x).wait()
        total = acc[...] + part_in[x]
        for b in range(received):
            z_copy(x + 2**b, b).wait()
            total = total + z_in[x + 2**b].astype(F32)
        return total

    for b in range(bits):
        count = zs // 2 ** (b + 1)

        def stage(j, carry, b=b, count=count):
            x = (2 * (count - 1 - j) + 1) * 2**b
            z_out[x] = both(x, b).astype(BF16)
            z_copy(x, b).start()
            return carry

        lax.fori_loop(0, count, stage, 0)
    sketch = both(0, bits)
    sk_ref[...] = sketch
    chosen = pick_columns(split3(sketch), leaf_ref[...])
    ch_ref[0] = chosen
    half = chosen.shape[0] // 2
    mine = pl.ds(pl.multiple_of(core * half, half), half)
    for s, p_ref in enumerate((p1_ref, p2_ref, p3_ref)):
        bit = col // 2**s % 2
        other = col + (1 - 2 * bit) * 2**s
        ex_out[s] = chosen
        if s == 0:
            copy = pltpu.make_async_remote_copy(
                src_ref=ex_out.at[s], dst_ref=ex_in.at[s],
                send_sem=ex_send.at[s], recv_sem=ex_recv.at[s],
                device_id=(row, other), device_id_type=MESH,
            )
            copy.start()
        else:
            copy = pltpu.make_async_remote_copy(
                src_ref=ex_out.at[s, mine], dst_ref=ex_in.at[s, mine],
                send_sem=ex_send.at[s], recv_sem=ex_recv.at[s],
                device_id=(row, other), device_id_type=MESH,
            )
            copy.start()
        if s == LEVELS - 1:
            inverse = shifted_inverses(
                [contract0(ch_ref[m], ch_ref[m]) for m in range(LEVELS)]
            )
            for m in range(LEVELS):
                inv_ref[m] = inverse[m]
        copy.wait()
        if s > 0:
            relay = pltpu.make_async_remote_copy(
                src_ref=ex_in.at[s, mine], dst_ref=ex_in.at[s, mine],
                send_sem=pass_send.at[s], recv_sem=pass_recv.at[s],
                device_id=(row, partner), device_id_type=MESH,
            )
            relay.start()
            relay.wait()
        theirs = ex_in[s]
        high = bit == 1
        low_part = jnp.where(high, theirs, chosen)
        high_part = jnp.where(high, chosen, theirs)
        cand = jnp.concatenate([low_part, high_part], axis=1)
        chosen = pick_columns(split3(cand), p_ref[pl.ds(me // 2 ** (s + 1), 1), :])
        ch_ref[s + 1] = chosen


def contract0(a, b):
    return lax.dot_general(
        a, b, (((0,), (0,)), ((), ())), precision=HIGHEST, preferred_element_type=F32
    )


def halves(x):
    h = x.astype(BF16)
    return h, (x - h.astype(F32)).astype(BF16)


def product3(a, b):
    ah, al = halves(a)
    bh, bl = halves(b)
    dot = functools.partial(jnp.dot, preferred_element_type=F32)
    return dot(ah, bh) + (dot(ah, bl) + dot(al, bh))


def product6(a, b):
    return jnp.dot(a, b, precision=HIGHEST, preferred_element_type=F32)


def shifted_inverses(grams):
    k = grams[0].shape[0]
    eye = lax.broadcasted_iota(jnp.int32, (k, k), 0) == lax.broadcasted_iota(
        jnp.int32, (k, k), 1
    )
    one = jnp.where(eye, 1.0, 0.0)
    low = 1.0 / (k / RIDGE + 1.0)
    gap = (1.0 - low) / (1.0 + low)
    first = 2.0 / (1.0 + low)
    tops, mats = [], []
    for gram in grams:
        trace = jnp.sum(jnp.where(eye, gram, 0.0), axis=(0, 1), keepdims=True)
        shift = RIDGE * (trace / k + 1e-06)
        tops.append(trace + shift)
        mats.append((gram + shift * one) / (trace + shift))
    scale = 2.0 / (2.0 - gap * gap)
    xs = [scale * (2.0 * first * one - first * first * m) for m in mats]
    gap = gap * gap / (2.0 - gap * gap)
    scales = []
    while gap > 1e-9:
        scales.append(2.0 / (2.0 - gap * gap))
        gap = gap * gap / (2.0 - gap * gap)
    for i, scale in enumerate(scales):
        product = product6 if i >= len(scales) - 2 else product3
        ys = [scale * (2.0 * one - product(m, x)) for m, x in zip(mats, xs)]
        xs = [product(x, y) for x, y in zip(xs, ys)]
    return [x / t for x, t in zip(xs, tops)]


def solve_kernel(sk_ref, ch_ref, inv_ref, o0, o1, o2, o3, root, r_ref, t_ref):
    col = lax.axis_index("col")
    levels = ch_ref.shape[0]
    top = ch_ref[levels - 1]
    inverse = [inv_ref[m] for m in range(levels - 1)] + shifted_inverses([contract0(top, top)])
    o0[...] = product6(contract0(sk_ref[...], ch_ref[0]), inverse[0])
    for s, o in enumerate((o1, o2, o3)):
        r_ref[...] = contract0(ch_ref[s], ch_ref[s + 1])
        size = o.shape[0]
        at = pl.multiple_of(col % 2**s * size, size)
        o[...] = product6(r_ref[pl.ds(at, size), :], inverse[s + 1])
    t_ref[...] = ch_ref[levels - 1].T
    size = root.shape[0]
    root[...] = t_ref[pl.ds(pl.multiple_of(col % 2**LEVELS * size, size), size), :]


def body(rows, cols, targets, sources, omega, tree_order, leaf_pivots, p1, p2, p3):
    n = rows * cols
    zs = cols // 2
    leaf = tree_order.shape[0]
    width = omega.shape[0]
    k = leaf_pivots.shape[1]
    per = targets.size // LANES
    vmem = pl.BlockSpec(memory_space=pltpu.VMEM)
    hbm = pl.BlockSpec(memory_space=pltpu.HBM)
    dma = lambda *d: pltpu.SemaphoreType.DMA(d)
    held = lambda a: pltpu.VMEM(a.shape, a.dtype)
    sketch, chosen, inverse = pl.pallas_call(
        functools.partial(sketch_kernel, rows, cols),
        out_shape=(
            jax.ShapeDtypeStruct((width, leaf), F32),
            jax.ShapeDtypeStruct((LEVELS + 1, width, k), F32),
            jax.ShapeDtypeStruct((LEVELS, k, k), F32),
        ),
        in_specs=[hbm] * 8,
        out_specs=(vmem,) * 3,
        scratch_shapes=[
            held(sources), held(omega), held(leaf_pivots), held(p1), held(p2), held(p3),
            pltpu.VMEM((n, 2, targets.shape[1]), F32),
            pltpu.VMEM((cols, 1, leaf), jnp.int32),
            pltpu.VMEM((3, LANES, n * per), BF16),
            pltpu.VMEM((sources.shape[1], SIDE), BF16),
            pltpu.VMEM((width, leaf), F32),
            pltpu.VMEM((zs, width, leaf), F32),
            pltpu.VMEM((zs, width, leaf), F32),
            pltpu.VMEM((zs, width, leaf), BF16),
            pltpu.VMEM((zs, width, leaf), BF16),
            pltpu.VMEM((LEVELS, width, k), F32),
            pltpu.VMEM((LEVELS, width, k), F32),
            dma(8),
            dma(n), dma(n), dma(cols), dma(cols), dma(zs), dma(zs), dma(zs), dma(zs),
            dma(LEVELS), dma(LEVELS), dma(LEVELS), dma(LEVELS),
        ],
        compiler_params=pltpu.CompilerParams(
            collective_id=0, has_side_effects=True, vmem_limit_bytes=56 << 20
        ),
    )(targets, sources, omega, tree_order.reshape(1, leaf), leaf_pivots, p1, p2, p3)
    out_rows = [leaf] + [k // 2**s for s in range(LEVELS)]
    return pl.pallas_call(
        solve_kernel,
        out_shape=tuple(jax.ShapeDtypeStruct((r, k), F32) for r in out_rows)
        + (jax.ShapeDtypeStruct((k // 2**LEVELS, width), F32),),
        in_specs=[vmem] * 3,
        out_specs=(vmem,) * (len(out_rows) + 1),
        scratch_shapes=[
            pltpu.VMEM((k, k), F32),
            pltpu.VMEM((k, width), F32),
        ],
        compiler_params=pltpu.CompilerParams(vmem_limit_bytes=32 << 20),
    )(sketch, chosen, inverse)


def solution(mesh):
    both = P(("row", "col"), None)
    return jax.shard_map(
        functools.partial(body, mesh.shape["row"], mesh.shape["col"]),
        mesh=mesh,
        in_specs=(
            P(None, ("row", "col")),
            P(None, "col"),
            P(None, "col"),
            P(("row", "col")),
            both,
            P(),
            P(),
            P(),
        ),
        out_specs=(both,) * 5,
        check_vma=False,
    )
```

```python
import functools

import jax
import jax.numpy as jnp
from jax import lax
from jax.experimental import pallas as pl
from jax.experimental.pallas import tpu as pltpu
from jax.sharding import PartitionSpec as P

RIDGE = 0.1
DELTA_SQUARED = 0.0001
LEVELS = 3
LANES = 128
CHUNK = 512
SIDE = 24
LN2 = 0.6931471805599453
MESH = pl.DeviceIdType.MESH
HIGHEST = lax.Precision.HIGHEST
F32 = jnp.float32
BF16 = jnp.bfloat16


def split3(x):
    a = x.astype(BF16)
    r = x - a.astype(F32)
    b = r.astype(BF16)
    c = (r - b.astype(F32)).astype(BF16)
    return a, b, c


def pick_columns(pieces, pivots):
    m = pieces[0].shape[1]
    hot = (
        lax.broadcasted_iota(jnp.int32, (m, pivots.shape[1]), 0) == pivots
    ).astype(F32).astype(BF16)
    out = None
    for piece in pieces:
        term = jnp.dot(piece, hot, preferred_element_type=F32)
        out = term if out is None else out + term
    return out


def flip(value, mask, bits):
    out = 0
    for i in range(bits):
        out = out + (value // 2**i + mask // 2**i) % 2 * 2**i
    return out


def sketch_kernel(
    rows, cols,
    tgt_hbm, src_hbm, om_hbm, ord_hbm, leaf_hbm, p1_hbm, p2_hbm, p3_hbm,
    sk_hbm, ch_ref, inv_ref,
    src_ref, om_ref, leaf_ref, p1_ref, p2_ref, p3_ref,
    every, orders, table, src_left, acc, part_out, part_in, z_out, z_in, ex_out, ex_in,
    load_sem,
    tgt_send, tgt_recv, ord_send, ord_recv, part_send, part_recv, z_send, z_recv,
    ex_send, ex_recv, pass_send, pass_recv,
):
    n = rows * cols
    zs = cols // 2
    bits = zs.bit_length() - 1
    row = lax.axis_index("row")
    col = lax.axis_index("col")
    me = row * cols + col
    z = col // 2
    core = col % 2
    partner = z * 2 + (1 - core)
    length = ord_hbm.shape[1]
    local = tgt_hbm.shape[1]
    per = 2 * local // LANES

    loads = [
        pltpu.make_async_copy(src, dst, load_sem.at[i])
        for i, (src, dst) in enumerate(
            (
                (src_hbm, src_ref), (om_hbm, om_ref), (leaf_hbm, leaf_ref),
                (p1_hbm, p1_ref), (p2_hbm, p2_ref), (p3_hbm, p3_ref),
                (tgt_hbm, every.at[me]), (ord_hbm, orders.at[col]),
            )
        )
    ]
    for load in loads:
        load.start()

    barrier = pltpu.get_barrier_semaphore()

    def greet(i, carry):
        other = lax.rem(me + i, n)
        pl.semaphore_signal(
            barrier, inc=1, device_id=(other // cols, other % cols), device_id_type=MESH
        )
        return carry

    lax.fori_loop(1, n, greet, 0)
    pl.semaphore_wait(barrier, n - 1)

    def tgt_copy(i):
        other = lax.rem(me + i, n)
        return pltpu.make_async_remote_copy(
            src_ref=tgt_hbm, dst_ref=every.at[me],
            send_sem=tgt_send.at[i], recv_sem=tgt_recv.at[i],
            device_id=(other // cols, other % cols), device_id_type=MESH,
        )

    def ord_copy(i):
        other = lax.rem(col + i, cols)
        return pltpu.make_async_remote_copy(
            src_ref=ord_hbm, dst_ref=orders.at[col],
            send_sem=ord_send.at[i], recv_sem=ord_recv.at[i],
            device_id=(row, other), device_id_type=MESH,
        )

    def start(copy):
        def go(i, carry):
            copy(i).start()
            return carry
        return go

    def finish(copy):
        def go(i, carry):
            copy(i).wait()
            return carry
        return go

    lax.fori_loop(1, n, start(tgt_copy), 0)
    lax.fori_loop(1, cols, start(ord_copy), 0)
    for load in loads:
        load.wait()

    def pieces(x):
        return [p.astype(F32) for p in split3(x)]

    wide = src_ref[...].astype(F32) - 0.5
    sx, sy = wide[0:1], wide[1:2]
    ones = jnp.ones_like(sx)
    left = []
    for part in (-2.0 * sx, -2.0 * sy):
        a, b, c = pieces(part)
        left += [a, a, a, b, b, c]
    left += pieces(sx * sx + sy * sy) + [ones] * 3
    left += [jnp.zeros_like(sx)] * (SIDE - len(left))
    src_left[...] = jnp.concatenate(left, axis=0).T.astype(BF16)

    lax.fori_loop(1, n, finish(tgt_copy), 0)
    lax.fori_loop(1, cols, finish(ord_copy), 0)

    flat = jnp.concatenate(
        [
            every[:, c, a * LANES : (a + 1) * LANES]
            for a in range(local // LANES)
            for c in range(2)
        ],
        axis=0,
    ).T
    for i, piece in enumerate(split3(flat)):
        table[i] = piece

    def points_of(leaf):
        order = orders[leaf]
        owner_row = order // LANES % (local // LANES) * (2 * n) + order // local
        lane = order % LANES
        rows_iota = lax.broadcasted_iota(jnp.int32, (n * per, length), 0)
        lane_iota = lax.broadcasted_iota(jnp.int32, (LANES, length), 0)
        out = []
        for c in range(2):
            hot = (rows_iota == owner_row + c * n).astype(F32).astype(BF16)
            got = jnp.dot(table[0], hot, preferred_element_type=F32)
            got += jnp.dot(table[1], hot, preferred_element_type=F32)
            got += jnp.dot(table[2], hot, preferred_element_type=F32)
            out.append(jnp.sum(jnp.where(lane_iota == lane, got, 0.0), axis=0, keepdims=True))
        return out

    sources = src_ref.shape[1]

    def block(leaf):
        px, py = points_of(leaf)
        px, py = px - 0.5, py - 0.5
        right = []
        for part in (px, py):
            a, b, c = pieces(part)
            right += [a, b, c, a, b, a]
        right += [jnp.ones_like(px)] * 3 + pieces(px * px + py * py + DELTA_SQUARED)
        right += [jnp.zeros_like(px)] * (SIDE - len(right))
        points = jnp.concatenate(right, axis=0).astype(BF16)

        def squares(at):
            return jnp.dot(
                src_left[at : at + CHUNK, :], points, preferred_element_type=F32
            )

        total = None
        ahead = squares(0)
        for at in range(0, sources, CHUNK):
            now = ahead
            if at + CHUNK < sources:
                ahead = squares(at + CHUNK)
            panel = ((-0.5 * LN2) * jnp.log2(now)).astype(BF16)
            term = jnp.dot(
                om_ref[:, at : at + CHUNK], panel, preferred_element_type=F32
            )
            total = term if total is None else total + term
        acc[...] = total

    def part_copy(x):
        return pltpu.make_async_remote_copy(
            src_ref=part_out.at[x], dst_ref=part_in.at[x],
            send_sem=part_send.at[x], recv_sem=part_recv.at[x],
            device_id=(row, partner), device_id_type=MESH,
        )

    def z_copy(x, b):
        return pltpu.make_async_remote_copy(
            src_ref=z_out.at[x], dst_ref=z_in.at[x],
            send_sem=z_send.at[x], recv_sem=z_recv.at[x],
            device_id=(row, flip(z, 2**b, bits) * 2 + core), device_id_type=MESH,
        )

    def both(x, received):
        to = flip(z, x, bits)
        block(to * 2 + (1 - core))
        part_out[x] = acc[...]
        part_copy(x).start()
        block(to * 2 + core)
        part_copy(x).wait()
        total = acc[...] + part_in[x]
        for b in range(received):
            z_copy(x + 2**b, b).wait()
            total = total + z_in[x + 2**b].astype(F32)
        return total

    for b in range(bits):
        count = zs // 2 ** (b + 1)

        def stage(j, carry, b=b, count=count):
            x = (2 * (count - 1 - j) + 1) * 2**b
            z_out[x] = both(x, b).astype(BF16)
            z_copy(x, b).start()
            return carry

        lax.fori_loop(0, count, stage, 0)
    sketch = both(0, bits)
    acc[...] = sketch
    keep = pltpu.make_async_copy(acc, sk_hbm, load_sem.at[0])
    keep.start()
    chosen = pick_columns(split3(sketch), leaf_ref[...])
    ch_ref[0] = chosen
    half = chosen.shape[0] // 2
    mine = pl.ds(pl.multiple_of(core * half, half), half)
    for s, p_ref in enumerate((p1_ref, p2_ref, p3_ref)):
        bit = col // 2**s % 2
        other = col + (1 - 2 * bit) * 2**s
        ex_out[s] = chosen
        if s == 0:
            copy = pltpu.make_async_remote_copy(
                src_ref=ex_out.at[s], dst_ref=ex_in.at[s],
                send_sem=ex_send.at[s], recv_sem=ex_recv.at[s],
                device_id=(row, other), device_id_type=MESH,
            )
            copy.start()
        else:
            copy = pltpu.make_async_remote_copy(
                src_ref=ex_out.at[s, mine], dst_ref=ex_in.at[s, mine],
                send_sem=ex_send.at[s], recv_sem=ex_recv.at[s],
                device_id=(row, other), device_id_type=MESH,
            )
            copy.start()
        if s == LEVELS - 1:
            inverse = shifted_inverses(
                [contract0(ch_ref[m], ch_ref[m]) for m in range(LEVELS)]
            )
            for m in range(LEVELS):
                inv_ref[m] = inverse[m]
        copy.wait()
        if s > 0:
            relay = pltpu.make_async_remote_copy(
                src_ref=ex_in.at[s, mine], dst_ref=ex_in.at[s, mine],
                send_sem=pass_send.at[s], recv_sem=pass_recv.at[s],
                device_id=(row, partner), device_id_type=MESH,
            )
            relay.start()
            relay.wait()
        theirs = ex_in[s]
        high = bit == 1
        low_part = jnp.where(high, theirs, chosen)
        high_part = jnp.where(high, chosen, theirs)
        cand = jnp.concatenate([low_part, high_part], axis=1)
        chosen = pick_columns(split3(cand), p_ref[pl.ds(me // 2 ** (s + 1), 1), :])
        ch_ref[s + 1] = chosen
    keep.wait()


def contract0(a, b):
    return lax.dot_general(
        a, b, (((0,), (0,)), ((), ())), precision=HIGHEST, preferred_element_type=F32
    )


def halves(x):
    h = x.astype(BF16)
    return h, (x - h.astype(F32)).astype(BF16)


def product3(a, b):
    ah, al = halves(a)
    bh, bl = halves(b)
    dot = functools.partial(jnp.dot, preferred_element_type=F32)
    return dot(ah, bh) + (dot(ah, bl) + dot(al, bh))


def product6(a, b):
    return jnp.dot(a, b, precision=HIGHEST, preferred_element_type=F32)


def shifted_inverses(grams):
    k = grams[0].shape[0]
    eye = lax.broadcasted_iota(jnp.int32, (k, k), 0) == lax.broadcasted_iota(
        jnp.int32, (k, k), 1
    )
    one = jnp.where(eye, 1.0, 0.0)
    low = 1.0 / (k / RIDGE + 1.0)
    gap = (1.0 - low) / (1.0 + low)
    first = 2.0 / (1.0 + low)
    tops, mats = [], []
    for gram in grams:
        trace = jnp.sum(jnp.where(eye, gram, 0.0), axis=(0, 1), keepdims=True)
        shift = RIDGE * (trace / k + 1e-06)
        tops.append(trace + shift)
        mats.append((gram + shift * one) / (trace + shift))
    scale = 2.0 / (2.0 - gap * gap)
    xs = [scale * (2.0 * first * one - first * first * m) for m in mats]
    gap = gap * gap / (2.0 - gap * gap)
    scales = []
    while gap > 1e-9:
        scales.append(2.0 / (2.0 - gap * gap))
        gap = gap * gap / (2.0 - gap * gap)
    for i, scale in enumerate(scales):
        product = product6 if i >= len(scales) - 2 else product3
        ys = [scale * (2.0 * one - product(m, x)) for m, x in zip(mats, xs)]
        xs = [product(x, y) for x, y in zip(xs, ys)]
    return [x / t for x, t in zip(xs, tops)]


def solve_kernel(
    sk_hbm, ch_hbm, inv_hbm, o0, o1, o2, o3, root, sk_ref, ch_ref, inv_ref, r_ref, t_ref, sem
):
    loads = [
        pltpu.make_async_copy(src, dst, sem.at[i])
        for i, (src, dst) in enumerate(
            ((ch_hbm, ch_ref), (sk_hbm, sk_ref), (inv_hbm, inv_ref))
        )
    ]
    for load in loads:
        load.start()
    for load in loads:
        load.wait()
    col = lax.axis_index("col")
    levels = ch_ref.shape[0]
    top = ch_ref[levels - 1]
    inverse = [inv_ref[m] for m in range(levels - 1)] + shifted_inverses([contract0(top, top)])
    o0[...] = product6(contract0(sk_ref[...], ch_ref[0]), inverse[0])
    for s, o in enumerate((o1, o2, o3)):
        r_ref[...] = contract0(ch_ref[s], ch_ref[s + 1])
        size = o.shape[0]
        at = pl.multiple_of(col % 2**s * size, size)
        o[...] = product6(r_ref[pl.ds(at, size), :], inverse[s + 1])
    t_ref[...] = ch_ref[levels - 1].T
    size = root.shape[0]
    root[...] = t_ref[pl.ds(pl.multiple_of(col % 2**LEVELS * size, size), size), :]


def body(rows, cols, targets, sources, omega, tree_order, leaf_pivots, p1, p2, p3):
    n = rows * cols
    zs = cols // 2
    leaf = tree_order.shape[0]
    width = omega.shape[0]
    k = leaf_pivots.shape[1]
    per = targets.size // LANES
    vmem = pl.BlockSpec(memory_space=pltpu.VMEM)
    hbm = pl.BlockSpec(memory_space=pltpu.HBM)
    dma = lambda *d: pltpu.SemaphoreType.DMA(d)
    held = lambda a: pltpu.VMEM(a.shape, a.dtype)
    sketch, chosen, inverse = pl.pallas_call(
        functools.partial(sketch_kernel, rows, cols),
        out_shape=(
            jax.ShapeDtypeStruct((width, leaf), F32),
            jax.ShapeDtypeStruct((LEVELS + 1, width, k), F32),
            jax.ShapeDtypeStruct((LEVELS, k, k), F32),
        ),
        in_specs=[hbm] * 8,
        out_specs=(hbm, vmem, vmem),
        scratch_shapes=[
            held(sources), held(omega), held(leaf_pivots), held(p1), held(p2), held(p3),
            pltpu.VMEM((n, 2, targets.shape[1]), F32),
            pltpu.VMEM((cols, 1, leaf), jnp.int32),
            pltpu.VMEM((3, LANES, n * per), BF16),
            pltpu.VMEM((sources.shape[1], SIDE), BF16),
            pltpu.VMEM((width, leaf), F32),
            pltpu.VMEM((zs, width, leaf), F32),
            pltpu.VMEM((zs, width, leaf), F32),
            pltpu.VMEM((zs, width, leaf), BF16),
            pltpu.VMEM((zs, width, leaf), BF16),
            pltpu.VMEM((LEVELS, width, k), F32),
            pltpu.VMEM((LEVELS, width, k), F32),
            dma(8),
            dma(n), dma(n), dma(cols), dma(cols), dma(zs), dma(zs), dma(zs), dma(zs),
            dma(LEVELS), dma(LEVELS), dma(LEVELS), dma(LEVELS),
        ],
        compiler_params=pltpu.CompilerParams(
            collective_id=0, has_side_effects=True, vmem_limit_bytes=56 << 20
        ),
    )(targets, sources, omega, tree_order.reshape(1, leaf), leaf_pivots, p1, p2, p3)
    out_rows = [leaf] + [k // 2**s for s in range(LEVELS)]
    return pl.pallas_call(
        solve_kernel,
        out_shape=tuple(jax.ShapeDtypeStruct((r, k), F32) for r in out_rows)
        + (jax.ShapeDtypeStruct((k // 2**LEVELS, width), F32),),
        in_specs=[hbm] * 3,
        out_specs=(vmem,) * (len(out_rows) + 1),
        scratch_shapes=[
            held(sketch), held(chosen), held(inverse),
            pltpu.VMEM((k, k), F32),
            pltpu.VMEM((k, width), F32),
            dma(3),
        ],
        compiler_params=pltpu.CompilerParams(vmem_limit_bytes=32 << 20),
    )(sketch, chosen, inverse)


def solution(mesh):
    both = P(("row", "col"), None)
    return jax.shard_map(
        functools.partial(body, mesh.shape["row"], mesh.shape["col"]),
        mesh=mesh,
        in_specs=(
            P(None, ("row", "col")),
            P(None, "col"),
            P(None, "col"),
            P(("row", "col")),
            both,
            P(),
            P(),
            P(),
        ),
        out_specs=(both,) * 5,
        check_vma=False,
    )
```
